32 devices in a mesh: crow: 2 (over y), ccol: 8 (over z, x), half: 2 (over core).
Axes of the slice: x: 2, y: 2, z: 4, core: 2. Of those that a mesh axis runs over, the one named last changes fastest.
Arguments:
- operator: bfloat16 [2, 8, 2048, 2048], P('crow', 'ccol', 'half'), may hold values from -0.09375 to 0.09375
- east_sources: bfloat16 [2, 8, 384, 2048], P('crow', 'ccol', None, 'half'), may hold values from -6 to 6
- west_sources: bfloat16 [2, 8, 384, 2048], P('crow', 'ccol', None, 'half'), may hold values from -6 to 6
Outputs:
- east_traces: bfloat16 [2, 8, 384, 2048], P('crow', 'ccol', None, 'half')
- west_traces: bfloat16 [2, 8, 384, 2048], P('crow', 'ccol', None, 'half')
The draws below stay inside these ranges and needn't reach their ends.
All inputs are finite; a program needn't handle non-finite values.
Results may differ from the reference program's by a relative error of at most 0.025.
Values may be sent and summed in bfloat16 or wider, within the bound.
A program may use at most 64 MiB of HBM per device.

```python
import jax
import jax.numpy as jnp
from jax import lax

TRACE = 2048
BATCH = 384
CELL_ROWS = 2
CELL_COLS = 8


def shard_levels(stream_key, dims, shards, least, top_value):
    gain, own = 1.0, jax.random.fold_in(stream_key, 6)
    for dim, blocks in shards:
        draws = jnp.exp(jax.random.uniform(jax.random.fold_in(own, dim), (blocks,), jnp.float32, least / len(shards), top_value / len(shards)))
        gain = gain * jnp.repeat(draws, dims[dim] // blocks).reshape([-1 if axis == dim else 1 for axis in range(len(dims))])
    return gain


def centred(stream_key, shape, deviation, bound, shards=(), kind=jnp.bfloat16):
    factor_of = shard_levels(stream_key, shape, shards, -0.22, 0.18) if shards else 1.0
    drawn = jax.random.normal(stream_key, shape, jnp.float32) * deviation * factor_of
    return jnp.minimum(jnp.maximum(drawn, -bound), bound).astype(kind)


def setup_inputs(seed: int = 0) -> dict:
    key_of = jax.random.split(jax.random.key(seed), 4)
    return {
        "operator": centred(key_of[0], (CELL_ROWS, CELL_COLS, TRACE, TRACE), (2 * TRACE) ** -0.5, 0.09375, ((0, 2), (1, 8), (2, 2))),
        "east_sources": centred(key_of[1], (CELL_ROWS, CELL_COLS, BATCH, TRACE), 1.0, 6.0, ((0, 2), (1, 8), (3, 2))),
        "west_sources": centred(key_of[2], (CELL_ROWS, CELL_COLS, BATCH, TRACE), 1.0, 6.0, ((0, 2), (1, 8), (3, 2))),
    }


def sweep_one(operator, sources, transpose):
    cols_total = operator.shape[1]
    batch_rows = sources.shape[2]
    trace_width = sources.shape[3]

    def row_step(upper_row, row_inputs):
        op_row, source_row = row_inputs

        def cell_step(western, inputs):
            matrix, source, from_north = inputs
            inflow = (from_north.astype(jnp.float32) + western.astype(jnp.float32)).astype(jnp.bfloat16)
            inflow = lax.optimization_barrier(inflow).astype(jnp.float32)
            dense = matrix.astype(jnp.float32)
            if transpose:
                dense = dense.T
            product = jnp.dot(inflow, dense, precision=lax.Precision.HIGHEST)
            newest = (product + source.astype(jnp.float32)).astype(jnp.bfloat16)
            return newest, newest

        start_west = jnp.zeros((batch_rows, trace_width), jnp.bfloat16)
        _, row_out = lax.scan(cell_step, start_west, (op_row, source_row, upper_row))
        return row_out, row_out

    start_row = jnp.zeros((cols_total, batch_rows, trace_width), jnp.bfloat16)
    _, traces = lax.scan(row_step, start_row, (operator, sources))
    return traces


def reference(operator, east_sources, west_sources):
    east_traces = sweep_one(operator, east_sources, True)
    flipped_op = jnp.flip(operator, axis=(0, 1))
    flipped_src = jnp.flip(west_sources, axis=(0, 1))
    west_traces = jnp.flip(sweep_one(flipped_op, flipped_src, False), axis=(0, 1))
    return east_traces, west_traces
```

```python
import functools

import jax
import jax.numpy as jnp
from jax import lax
from jax.experimental import pallas as pl
from jax.experimental.pallas import tpu as pltpu
from jax.sharding import PartitionSpec as P

BLOCKS = 12
MESH = pl.DeviceIdType.MESH


def sweeps(rows, cols, op_ref, es_ref, ws_ref, eo_ref, wo_ref,
           op, op_t, es, ws, eout, wout, e_north, e_west, w_south, w_east,
           e_in, e_sib, w_part, w_sib, w_in, e_acc,
           load_sem, store_sem, send_sem, en_sem, ew_sem, wsn_sem, we_sem, esib_sem, wsib_sem):
    row, col, half = lax.axis_index("crow"), lax.axis_index("ccol"), lax.axis_index("half")
    blocks, block_rows, width = es.shape
    tile = min(256, width)
    east_level = row + col
    west_level = rows - 1 - row + cols - 1 - col
    has_n, has_s, has_w, has_e = row > 0, row < rows - 1, col > 0, col < cols - 1
    north, south = {"crow": row - 1}, {"crow": row + 1}
    west, east = {"ccol": col - 1}, {"ccol": col + 1}
    other = {"half": 1 - half}

    own = pl.multiple_of(half * width, width)
    theirs = pl.multiple_of((1 - half) * width, width)
    loads = [
        pltpu.make_async_copy(es_ref, es, load_sem.at[0]),
        pltpu.make_async_copy(ws_ref, ws, load_sem.at[1]),
        pltpu.make_async_copy(op_ref.at[:, pl.ds(own, width)], op.at[0], load_sem.at[2]),
        pltpu.make_async_copy(op_ref.at[:, pl.ds(theirs, width)], op.at[1], load_sem.at[3]),
    ]
    for load in loads:
        load.start()

    barrier = pltpu.get_barrier_semaphore()
    pl.semaphore_signal(barrier, inc=1, device_id=other, device_id_type=MESH)
    for there, who in ((has_n, north), (has_s, south), (has_w, west), (has_e, east)):
        @pl.when(there)
        def _():
            pl.semaphore_signal(barrier, inc=1, device_id=who, device_id_type=MESH)
    for there, buffer in ((has_n, e_north), (has_s, w_south), (has_w, e_west), (has_e, w_east)):
        @pl.when(jnp.logical_not(there))
        def _():
            buffer[...] = jnp.zeros_like(buffer)
    pl.semaphore_wait(
        barrier,
        1 + has_n.astype(jnp.int32) + has_s.astype(jnp.int32)
        + has_w.astype(jnp.int32) + has_e.astype(jnp.int32),
    )

    def remote(src, dst, send, recv, who):
        return pltpu.make_async_remote_copy(
            src_ref=src, dst_ref=dst, send_sem=send, recv_sem=recv,
            device_id=who, device_id_type=MESH)

    def to_south(src, k):
        return remote(src.at[k], e_north.at[k], send_sem.at[0], en_sem.at[k], south)

    def to_east(src, k):
        return remote(src.at[k], e_west.at[k], send_sem.at[1], ew_sem.at[k], east)

    def to_north(src, k):
        return remote(src.at[k], w_south.at[k], send_sem.at[2], wsn_sem.at[k], north)

    def to_west(src, k):
        return remote(src.at[k], w_east.at[k], send_sem.at[3], we_sem.at[k], west)

    def e_exchange(k):
        return remote(e_in.at[k], e_sib.at[k], send_sem.at[4], esib_sem.at[k], other)

    def w_exchange(k):
        return remote(w_part.at[k], w_sib.at[k], send_sem.at[5], wsib_sem.at[k], other)

    def send_east(src, k):
        @pl.when(has_e)
        def _():
            to_east(src, k).start()

        @pl.when(has_s)
        def _():
            to_south(src, k).start()
        pltpu.make_async_copy(src.at[k], eo_ref.at[k], store_sem.at[0]).start()

    def send_west(src, k):
        @pl.when(has_w)
        def _():
            to_west(src, k).start()

        @pl.when(has_n)
        def _():
            to_north(src, k).start()
        pltpu.make_async_copy(src.at[k], wo_ref.at[k], store_sem.at[1]).start()

    loads[0].wait()

    @pl.when(east_level == 0)
    def _():
        @pl.loop(0, blocks)
        def _(k):
            send_east(es, k)

    loads[1].wait()

    @pl.when(west_level == 0)
    def _():
        @pl.loop(0, blocks)
        def _(k):
            send_west(ws, k)

    loads[2].wait()
    loads[3].wait()

    @pl.when(east_level > 0)
    def _():
        @pl.loop(0, width // tile)
        def _(t):
            at = pl.multiple_of(t * tile, tile)
            for k in range(2):
                for n in range(0, width, tile):
                    op_t[k, pl.ds(at, tile), n:n + tile] = op[k, n:n + tile, pl.ds(at, tile)].T

    @pl.loop(0, rows + cols - 2 + blocks)
    def _(step):
        ek, wk = step - east_level, step - west_level
        e_on = (east_level > 0) & (ek >= 0) & (ek < blocks)
        w_on = (west_level > 0) & (wk >= 0) & (wk < blocks)

        @pl.when(e_on)
        def _():
            @pl.when(has_n)
            def _():
                to_south(eout, ek).wait_recv()

            @pl.when(has_w)
            def _():
                to_east(eout, ek).wait_recv()
            e_in[ek] = (e_north[ek].astype(jnp.float32) + e_west[ek].astype(jnp.float32)).astype(jnp.bfloat16)
            e_exchange(ek).start()

        @pl.when(w_on)
        def _():
            @pl.when(has_s)
            def _():
                to_north(wout, wk).wait_recv()

            @pl.when(has_e)
            def _():
                to_west(wout, wk).wait_recv()
            w_in[...] = (w_south[wk].astype(jnp.float32) + w_east[wk].astype(jnp.float32)).astype(jnp.bfloat16)
            for n in range(0, width, tile):
                w_part[wk, :, n:n + tile] = jnp.dot(
                    w_in[...], op[1, :, n:n + tile], preferred_element_type=jnp.float32).astype(jnp.bfloat16)
            w_exchange(wk).start()

        @pl.when(e_on)
        def _():
            for n in range(0, width, tile):
                e_acc[:, n:n + tile] = es[ek, :, n:n + tile].astype(jnp.float32) + jnp.dot(
                    e_in[ek], op_t[0, :, n:n + tile], preferred_element_type=jnp.float32)
            e_exchange(ek).wait_recv()
            for n in range(0, width, tile):
                eout[ek, :, n:n + tile] = (e_acc[:, n:n + tile] + jnp.dot(
                    e_sib[ek], op_t[1, :, n:n + tile], preferred_element_type=jnp.float32)).astype(jnp.bfloat16)
            send_east(eout, ek)

        @pl.when(w_on)
        def _():
            for n in range(0, width, tile):
                e_acc[:, n:n + tile] = ws[wk, :, n:n + tile].astype(jnp.float32) + jnp.dot(
                    w_in[...], op[0, :, n:n + tile], preferred_element_type=jnp.float32)
            w_exchange(wk).wait_recv()
            wout[wk] = (e_acc[...] + w_sib[wk].astype(jnp.float32)).astype(jnp.bfloat16)
            send_west(wout, wk)

    for there, src, dst, send, recv, who in (
        (has_s, eout, e_north, 0, en_sem, south),
        (has_e, eout, e_west, 1, ew_sem, east),
        (has_n, wout, w_south, 2, wsn_sem, north),
        (has_w, wout, w_east, 3, we_sem, west),
        (east_level > 0, e_in, e_sib, 4, esib_sem, other),
        (west_level > 0, w_part, w_sib, 5, wsib_sem, other),
    ):
        @pl.when(there)
        def _():
            remote(src, dst, send_sem.at[send], recv.at[0], who).wait_send()
    pltpu.make_async_copy(eout, eo_ref, store_sem.at[0]).wait()
    pltpu.make_async_copy(wout, wo_ref, store_sem.at[1]).wait()


def local(rows, cols, operator, east_sources, west_sources):
    matrix = operator[0, 0]
    batch, width = east_sources.shape[2:]
    blocks, block_rows = BLOCKS, batch // BLOCKS
    cut = (blocks, block_rows, width)
    any_space = pl.BlockSpec(memory_space=pl.ANY)
    trace = pltpu.VMEM(cut, jnp.bfloat16)
    weights = pltpu.VMEM((2, width, width), jnp.bfloat16)
    east, west = pl.pallas_call(
        functools.partial(sweeps, rows, cols),
        out_shape=[jax.ShapeDtypeStruct(cut, jnp.bfloat16)] * 2,
        in_specs=[any_space] * 3,
        out_specs=[any_space] * 2,
        scratch_shapes=[weights, weights] + [trace] * 12 + [
            pltpu.VMEM((block_rows, width), jnp.bfloat16),
            pltpu.VMEM((block_rows, width), jnp.float32),
            pltpu.SemaphoreType.DMA((4,)),
            pltpu.SemaphoreType.DMA((2,)),
            pltpu.SemaphoreType.DMA((6,)),
        ] + [pltpu.SemaphoreType.DMA((blocks,))] * 6,
        compiler_params=pltpu.CompilerParams(
            collective_id=0, has_side_effects=True, vmem_limit_bytes=40 * 2**20),
        name="sweeps",
    )(matrix, east_sources.reshape(cut), west_sources.reshape(cut))
    return east.reshape(1, 1, batch, width), west.reshape(1, 1, batch, width)


def solution(mesh):
    in_specs = (
        P("crow", "ccol", "half", None),
        P("crow", "ccol", None, "half"),
        P("crow", "ccol", None, "half"),
    )
    out_specs = (P("crow", "ccol", None, "half"), P("crow", "ccol", None, "half"))
    body = functools.partial(local, mesh.shape["crow"], mesh.shape["ccol"])
    return jax.shard_map(body, mesh=mesh, in_specs=in_specs, out_specs=out_specs, check_vma=False)
```

```python
import functools

import jax
import jax.numpy as jnp
from jax import lax
from jax.experimental import pallas as pl
from jax.experimental.pallas import tpu as pltpu
from jax.sharding import PartitionSpec as P

BLOCKS = 12
SKEW = 4
MESH = pl.DeviceIdType.MESH


def sweeps(rows, cols, op_ref, es_ref, ws_ref, eo_ref, wo_ref,
           op, op_t, es, ws, eout, wout, e_north, e_west, w_south, w_east,
           e_in, e_sib, w_part, w_sib, w_in, e_acc,
           load_sem, store_sem, send_sem, en_sem, ew_sem, wsn_sem, we_sem, esib_sem, wsib_sem):
    row, col, half = lax.axis_index("crow"), lax.axis_index("ccol"), lax.axis_index("half")
    blocks, block_rows, width = es.shape
    tile = min(256, width)
    east_level = row + col
    west_level = rows - 1 - row + cols - 1 - col
    has_n, has_s, has_w, has_e = row > 0, row < rows - 1, col > 0, col < cols - 1
    north, south = {"crow": row - 1}, {"crow": row + 1}
    west, east = {"ccol": col - 1}, {"ccol": col + 1}
    other = {"half": 1 - half}

    own = pl.multiple_of(half * width, width)
    theirs = pl.multiple_of((1 - half) * width, width)
    loads = [
        pltpu.make_async_copy(es_ref, es, load_sem.at[0]),
        pltpu.make_async_copy(ws_ref, ws, load_sem.at[1]),
        pltpu.make_async_copy(op_ref.at[:, pl.ds(own, width)], op.at[0], load_sem.at[2]),
        pltpu.make_async_copy(op_ref.at[:, pl.ds(theirs, width)], op.at[1], load_sem.at[3]),
    ]
    for load in loads:
        load.start()

    barrier = pltpu.get_barrier_semaphore()
    pl.semaphore_signal(barrier, inc=1, device_id=other, device_id_type=MESH)
    for there, who in ((has_n, north), (has_s, south), (has_w, west), (has_e, east)):
        @pl.when(there)
        def _():
            pl.semaphore_signal(barrier, inc=1, device_id=who, device_id_type=MESH)
    for there, buffer in ((has_n, e_north), (has_s, w_south), (has_w, e_west), (has_e, w_east)):
        @pl.when(jnp.logical_not(there))
        def _():
            buffer[...] = jnp.zeros_like(buffer)
    pl.semaphore_wait(
        barrier,
        1 + has_n.astype(jnp.int32) + has_s.astype(jnp.int32)
        + has_w.astype(jnp.int32) + has_e.astype(jnp.int32),
    )

    def remote(src, dst, send, recv, who):
        return pltpu.make_async_remote_copy(
            src_ref=src, dst_ref=dst, send_sem=send, recv_sem=recv,
            device_id=who, device_id_type=MESH)

    def to_south(src, k):
        return remote(src.at[k], e_north.at[k], send_sem.at[0], en_sem.at[k], south)

    def to_east(src, k):
        return remote(src.at[k], e_west.at[k], send_sem.at[1], ew_sem.at[k], east)

    def to_north(src, k):
        return remote(src.at[k], w_south.at[k], send_sem.at[2], wsn_sem.at[k], north)

    def to_west(src, k):
        return remote(src.at[k], w_east.at[k], send_sem.at[3], we_sem.at[k], west)

    def e_exchange(k):
        return remote(e_in.at[k], e_sib.at[k], send_sem.at[4], esib_sem.at[k], other)

    def w_exchange(k):
        return remote(w_part.at[k], w_sib.at[k], send_sem.at[5], wsib_sem.at[k], other)

    def send_east(src, k):
        @pl.when(has_e)
        def _():
            to_east(src, k).start()

        @pl.when(has_s)
        def _():
            to_south(src, k).start()
        pltpu.make_async_copy(src.at[k], eo_ref.at[k], store_sem.at[0]).start()

    def send_west(src, k):
        @pl.when(has_w)
        def _():
            to_west(src, k).start()

        @pl.when(has_n)
        def _():
            to_north(src, k).start()
        pltpu.make_async_copy(src.at[k], wo_ref.at[k], store_sem.at[1]).start()

    loads[0].wait()

    @pl.when(east_level == 0)
    def _():
        @pl.loop(0, blocks)
        def _(k):
            send_east(es, k)

    loads[1].wait()

    @pl.when(west_level == 0)
    def _():
        @pl.loop(0, blocks)
        def _(k):
            send_west(ws, k)

    loads[2].wait()
    loads[3].wait()

    @pl.when(east_level > 0)
    def _():
        @pl.loop(0, width // tile)
        def _(t):
            at = pl.multiple_of(t * tile, tile)
            for k in range(2):
                for n in range(0, width, tile):
                    op_t[k, pl.ds(at, tile), n:n + tile] = op[k, n:n + tile, pl.ds(at, tile)].T

    @pl.loop(0, SKEW * (rows + cols - 2) + blocks)
    def _(step):
        ek, wk = step - SKEW * east_level, step - SKEW * west_level
        e_on = (east_level > 0) & (ek >= 0) & (ek < blocks)
        w_on = (west_level > 0) & (wk >= 0) & (wk < blocks)

        @pl.when(e_on)
        def _():
            @pl.when(has_n)
            def _():
                to_south(eout, ek).wait_recv()

            @pl.when(has_w)
            def _():
                to_east(eout, ek).wait_recv()
            e_in[ek] = (e_north[ek].astype(jnp.float32) + e_west[ek].astype(jnp.float32)).astype(jnp.bfloat16)
            e_exchange(ek).start()

        @pl.when(w_on)
        def _():
            @pl.when(has_s)
            def _():
                to_north(wout, wk).wait_recv()

            @pl.when(has_e)
            def _():
                to_west(wout, wk).wait_recv()
            w_in[...] = (w_south[wk].astype(jnp.float32) + w_east[wk].astype(jnp.float32)).astype(jnp.bfloat16)
            for n in range(0, width, tile):
                w_part[wk, :, n:n + tile] = jnp.dot(
                    w_in[...], op[1, :, n:n + tile], preferred_element_type=jnp.float32).astype(jnp.bfloat16)
            w_exchange(wk).start()

        @pl.when(e_on)
        def _():
            for n in range(0, width, tile):
                e_acc[:, n:n + tile] = es[ek, :, n:n + tile].astype(jnp.float32) + jnp.dot(
                    e_in[ek], op_t[0, :, n:n + tile], preferred_element_type=jnp.float32)
            e_exchange(ek).wait_recv()
            for n in range(0, width, tile):
                eout[ek, :, n:n + tile] = (e_acc[:, n:n + tile] + jnp.dot(
                    e_sib[ek], op_t[1, :, n:n + tile], preferred_element_type=jnp.float32)).astype(jnp.bfloat16)
            send_east(eout, ek)

        @pl.when(w_on)
        def _():
            for n in range(0, width, tile):
                e_acc[:, n:n + tile] = ws[wk, :, n:n + tile].astype(jnp.float32) + jnp.dot(
                    w_in[...], op[0, :, n:n + tile], preferred_element_type=jnp.float32)
            w_exchange(wk).wait_recv()
            wout[wk] = (e_acc[...] + w_sib[wk].astype(jnp.float32)).astype(jnp.bfloat16)
            send_west(wout, wk)

    for there, src, dst, send, recv, who in (
        (has_s, eout, e_north, 0, en_sem, south),
        (has_e, eout, e_west, 1, ew_sem, east),
        (has_n, wout, w_south, 2, wsn_sem, north),
        (has_w, wout, w_east, 3, we_sem, west),
        (east_level > 0, e_in, e_sib, 4, esib_sem, other),
        (west_level > 0, w_part, w_sib, 5, wsib_sem, other),
    ):
        @pl.when(there)
        def _():
            remote(src, dst, send_sem.at[send], recv.at[0], who).wait_send()
    pltpu.make_async_copy(eout, eo_ref, store_sem.at[0]).wait()
    pltpu.make_async_copy(wout, wo_ref, store_sem.at[1]).wait()


def local(rows, cols, operator, east_sources, west_sources):
    matrix = operator[0, 0]
    batch, width = east_sources.shape[2:]
    blocks, block_rows = BLOCKS, batch // BLOCKS
    cut = (blocks, block_rows, width)
    any_space = pl.BlockSpec(memory_space=pl.ANY)
    trace = pltpu.VMEM(cut, jnp.bfloat16)
    weights = pltpu.VMEM((2, width, width), jnp.bfloat16)
    east, west = pl.pallas_call(
        functools.partial(sweeps, rows, cols),
        out_shape=[jax.ShapeDtypeStruct(cut, jnp.bfloat16)] * 2,
        in_specs=[any_space] * 3,
        out_specs=[any_space] * 2,
        scratch_shapes=[weights, weights] + [trace] * 12 + [
            pltpu.VMEM((block_rows, width), jnp.bfloat16),
            pltpu.VMEM((block_rows, width), jnp.float32),
            pltpu.SemaphoreType.DMA((4,)),
            pltpu.SemaphoreType.DMA((2,)),
            pltpu.SemaphoreType.DMA((6,)),
        ] + [pltpu.SemaphoreType.DMA((blocks,))] * 6,
        compiler_params=pltpu.CompilerParams(
            collective_id=0, has_side_effects=True, vmem_limit_bytes=63 * 2**20),
        name="sweeps",
    )(matrix, east_sources.reshape(cut), west_sources.reshape(cut))
    return east.reshape(1, 1, batch, width), west.reshape(1, 1, batch, width)


def solution(mesh):
    in_specs = (
        P("crow", "ccol", "half", None),
        P("crow", "ccol", None, "half"),
        P("crow", "ccol", None, "half"),
    )
    out_specs = (P("crow", "ccol", None, "half"), P("crow", "ccol", None, "half"))
    body = functools.partial(local, mesh.shape["crow"], mesh.shape["ccol"])
    return jax.shard_map(body, mesh=mesh, in_specs=in_specs, out_specs=out_specs, check_vma=False)
```

```python
import functools

import jax
import jax.numpy as jnp
from jax import lax
from jax.experimental import pallas as pl
from jax.experimental.pallas import tpu as pltpu
from jax.sharding import PartitionSpec as P

BLOCKS = 8
SKEW = 4
DIRECT = 3
LAG = 2
MESH = pl.DeviceIdType.MESH


def sweeps(rows, cols, op_ref, es_ref, ws_ref, eo_ref, wo_ref,
           op, op_t, es, ws, eout, wout, e_north, e_west, w_south, w_east,
           e_in, e_sib, w_part, w_sib, e_relay, w_relay, w_in, e_acc,
           load_sem, store_sem, send_sem, en_sem, ew_sem, wsn_sem, we_sem, esib_sem, wsib_sem, er_sem, wr_sem):
    row, col, half = lax.axis_index("crow"), lax.axis_index("ccol"), lax.axis_index("half")
    blocks, block_rows, width = es.shape
    tile = min(256, width)
    east_level = row + col
    west_level = rows - 1 - row + cols - 1 - col
    has_n, has_s, has_w, has_e = row > 0, row < rows - 1, col > 0, col < cols - 1
    north, south = {"crow": row - 1}, {"crow": row + 1}
    west, east = {"ccol": col - 1}, {"ccol": col + 1}
    other = {"half": 1 - half}

    mid, last = cols // 2, cols - 1
    detour = mid >= 2
    e_from, e_via = detour & (col == mid - 1), detour & (col == 0)
    w_from, w_via = detour & (col == mid), detour & (col == last)
    at_mid, at_end = e_from | w_from, e_via | w_via

    own = pl.multiple_of(half * width, width)
    theirs = pl.multiple_of((1 - half) * width, width)
    loads = [
        pltpu.make_async_copy(es_ref, es, load_sem.at[0]),
        pltpu.make_async_copy(ws_ref, ws, load_sem.at[1]),
        pltpu.make_async_copy(op_ref.at[:, pl.ds(own, width)], op.at[0], load_sem.at[2]),
        pltpu.make_async_copy(op_ref.at[:, pl.ds(theirs, width)], op.at[1], load_sem.at[3]),
    ]
    for load in loads:
        load.start()

    barrier = pltpu.get_barrier_semaphore()
    pl.semaphore_signal(barrier, inc=1, device_id=other, device_id_type=MESH)
    for there, who in ((has_n, north), (has_s, south), (has_w, west), (has_e, east)):
        @pl.when(there)
        def _():
            pl.semaphore_signal(barrier, inc=1, device_id=who, device_id_type=MESH)
    for there, whos in ((at_mid, (0, last)), (at_end, (mid - 1, mid))):
        @pl.when(there)
        def _():
            for who in whos:
                pl.semaphore_signal(barrier, inc=1, device_id={"ccol": who}, device_id_type=MESH)
    for there, buffer in ((has_n, e_north), (has_s, w_south), (has_w, e_west), (has_e, w_east)):
        @pl.when(jnp.logical_not(there))
        def _():
            buffer[...] = jnp.zeros_like(buffer)
    pl.semaphore_wait(
        barrier,
        1 + has_n.astype(jnp.int32) + has_s.astype(jnp.int32)
        + has_w.astype(jnp.int32) + has_e.astype(jnp.int32)
        + 2 * at_mid.astype(jnp.int32) + 2 * at_end.astype(jnp.int32),
    )

    def remote(src, dst, send, recv, who):
        return pltpu.make_async_remote_copy(
            src_ref=src, dst_ref=dst, send_sem=send, recv_sem=recv,
            device_id=who, device_id_type=MESH)

    def to_south(src, k):
        return remote(src.at[k], e_north.at[k], send_sem.at[0], en_sem.at[k], south)

    def to_east(src, k):
        return remote(src.at[k], e_west.at[k], send_sem.at[1], ew_sem.at[k], east)

    def to_north(src, k):
        return remote(src.at[k], w_south.at[k], send_sem.at[2], wsn_sem.at[k], north)

    def to_west(src, k):
        return remote(src.at[k], w_east.at[k], send_sem.at[3], we_sem.at[k], west)

    def e_exchange(k):
        return remote(e_in.at[k], e_sib.at[k], send_sem.at[4], esib_sem.at[k], other)

    def w_exchange(k):
        return remote(w_part.at[k], w_sib.at[k], send_sem.at[5], wsib_sem.at[k], other)

    def e_out(k):
        return remote(eout.at[k], e_relay.at[k], send_sem.at[1], er_sem.at[k], {"ccol": 0})

    def e_on_to(k):
        return remote(e_relay.at[k], e_west.at[k], send_sem.at[6], ew_sem.at[k], {"ccol": mid})

    def w_out(k):
        return remote(wout.at[k], w_relay.at[k], send_sem.at[3], wr_sem.at[k], {"ccol": last})

    def w_on_to(k):
        return remote(w_relay.at[k], w_east.at[k], send_sem.at[7], we_sem.at[k], {"ccol": mid - 1})

    def send_east(src, k):
        far = e_from & (k >= DIRECT)
        if detour and src is eout:
            @pl.when(far)
            def _():
                e_out(k).start()

        @pl.when(has_e & jnp.logical_not(far))
        def _():
            to_east(src, k).start()

        @pl.when(has_s)
        def _():
            to_south(src, k).start()
        pltpu.make_async_copy(src.at[k], eo_ref.at[k], store_sem.at[0]).start()

    def send_west(src, k):
        far = w_from & (k >= DIRECT)
        if detour and src is wout:
            @pl.when(far)
            def _():
                w_out(k).start()

        @pl.when(has_w & jnp.logical_not(far))
        def _():
            to_west(src, k).start()

        @pl.when(has_n)
        def _():
            to_north(src, k).start()
        pltpu.make_async_copy(src.at[k], wo_ref.at[k], store_sem.at[1]).start()

    loads[0].wait()

    @pl.when(east_level == 0)
    def _():
        @pl.loop(0, blocks)
        def _(k):
            send_east(es, k)

    loads[1].wait()

    @pl.when(west_level == 0)
    def _():
        @pl.loop(0, blocks)
        def _(k):
            send_west(ws, k)

    loads[2].wait()
    loads[3].wait()

    @pl.when(east_level > 0)
    def _():
        @pl.loop(0, width // tile)
        def _(t):
            at = pl.multiple_of(t * tile, tile)
            for k in range(2):
                for n in range(0, width, tile):
                    op_t[k, pl.ds(at, tile), n:n + tile] = op[k, n:n + tile, pl.ds(at, tile)].T

    @pl.loop(0, SKEW * (rows + cols - 2) + blocks)
    def _(step):
        ek, wk = step - SKEW * east_level, step - SKEW * west_level
        e_on = (east_level > 0) & (ek >= 0) & (ek < blocks)
        w_on = (west_level > 0) & (wk >= 0) & (wk < blocks)

        if detour:
            er = step - SKEW * (row + mid - 1) - LAG
            wr = step - SKEW * (rows - 1 - row + last - mid) - LAG

            @pl.when(e_via & (er >= DIRECT) & (er < blocks))
            def _():
                e_out(er).wait_recv()
                e_on_to(er).start()

            @pl.when(w_via & (wr >= DIRECT) & (wr < blocks))
            def _():
                w_out(wr).wait_recv()
                w_on_to(wr).start()

        @pl.when(e_on)
        def _():
            @pl.when(has_n)
            def _():
                to_south(eout, ek).wait_recv()

            @pl.when(has_w)
            def _():
                to_east(eout, ek).wait_recv()
            e_in[ek] = (e_north[ek].astype(jnp.float32) + e_west[ek].astype(jnp.float32)).astype(jnp.bfloat16)
            e_exchange(ek).start()

        @pl.when(w_on)
        def _():
            @pl.when(has_s)
            def _():
                to_north(wout, wk).wait_recv()

            @pl.when(has_e)
            def _():
                to_west(wout, wk).wait_recv()
            w_in[...] = (w_south[wk].astype(jnp.float32) + w_east[wk].astype(jnp.float32)).astype(jnp.bfloat16)
            for n in range(0, width, tile):
                w_part[wk, :, n:n + tile] = jnp.dot(
                    w_in[...], op[1, :, n:n + tile], preferred_element_type=jnp.float32).astype(jnp.bfloat16)
            w_exchange(wk).start()

        @pl.when(e_on)
        def _():
            for n in range(0, width, tile):
                e_acc[:, n:n + tile] = es[ek, :, n:n + tile].astype(jnp.float32) + jnp.dot(
                    e_in[ek], op_t[0, :, n:n + tile], preferred_element_type=jnp.float32)
            e_exchange(ek).wait_recv()
            for n in range(0, width, tile):
                eout[ek, :, n:n + tile] = (e_acc[:, n:n + tile] + jnp.dot(
                    e_sib[ek], op_t[1, :, n:n + tile], preferred_element_type=jnp.float32)).astype(jnp.bfloat16)
            send_east(eout, ek)

        @pl.when(w_on)
        def _():
            for n in range(0, width, tile):
                e_acc[:, n:n + tile] = ws[wk, :, n:n + tile].astype(jnp.float32) + jnp.dot(
                    w_in[...], op[0, :, n:n + tile], preferred_element_type=jnp.float32)
            w_exchange(wk).wait_recv()
            wout[wk] = (e_acc[...] + w_sib[wk].astype(jnp.float32)).astype(jnp.bfloat16)
            send_west(wout, wk)

    for there, src, dst, send, recv, who in (
        (has_s, eout, e_north, 0, en_sem, south),
        (has_e, eout, e_west, 1, ew_sem, east),
        (has_n, wout, w_south, 2, wsn_sem, north),
        (has_w, wout, w_east, 3, we_sem, west),
        (east_level > 0, e_in, e_sib, 4, esib_sem, other),
        (west_level > 0, w_part, w_sib, 5, wsib_sem, other),
    ):
        @pl.when(there)
        def _():
            remote(src, dst, send_sem.at[send], recv.at[0], who).wait_send()
    if detour and DIRECT < blocks:
        for there, src, dst, send, recv, who in (
            (e_via, e_relay, e_west, 6, ew_sem, mid), (w_via, w_relay, w_east, 7, we_sem, mid - 1),
        ):
            @pl.when(there)
            def _():
                some = pl.ds(DIRECT, blocks - DIRECT)
                remote(src.at[some], dst.at[some], send_sem.at[send], recv.at[0], {"ccol": who}).wait_send()
    pltpu.make_async_copy(eout, eo_ref, store_sem.at[0]).wait()
    pltpu.make_async_copy(wout, wo_ref, store_sem.at[1]).wait()


def local(rows, cols, operator, east_sources, west_sources):
    matrix = operator[0, 0]
    batch, width = east_sources.shape[2:]
    blocks, block_rows = BLOCKS, batch // BLOCKS
    cut = (blocks, block_rows, width)
    any_space = pl.BlockSpec(memory_space=pl.ANY)
    trace = pltpu.VMEM(cut, jnp.bfloat16)
    weights = pltpu.VMEM((2, width, width), jnp.bfloat16)
    east, west = pl.pallas_call(
        functools.partial(sweeps, rows, cols),
        out_shape=[jax.ShapeDtypeStruct(cut, jnp.bfloat16)] * 2,
        in_specs=[any_space] * 3,
        out_specs=[any_space] * 2,
        scratch_shapes=[weights, weights] + [trace] * 14 + [
            pltpu.VMEM((block_rows, width), jnp.bfloat16),
            pltpu.VMEM((block_rows, width), jnp.float32),
            pltpu.SemaphoreType.DMA((4,)),
            pltpu.SemaphoreType.DMA((2,)),
            pltpu.SemaphoreType.DMA((8,)),
        ] + [pltpu.SemaphoreType.DMA((blocks,))] * 8,
        compiler_params=pltpu.CompilerParams(
            collective_id=0, has_side_effects=True, vmem_limit_bytes=63 * 2**20),
        name="sweeps",
    )(matrix, east_sources.reshape(cut), west_sources.reshape(cut))
    return east.reshape(1, 1, batch, width), west.reshape(1, 1, batch, width)


def solution(mesh):
    in_specs = (
        P("crow", "ccol", "half", None),
        P("crow", "ccol", None, "half"),
        P("crow", "ccol", None, "half"),
    )
    out_specs = (P("crow", "ccol", None, "half"), P("crow", "ccol", None, "half"))
    body = functools.partial(local, mesh.shape["crow"], mesh.shape["ccol"])
    return jax.shard_map(body, mesh=mesh, in_specs=in_specs, out_specs=out_specs, check_vma=False)
```
